512 devices in a mesh: member: 16 (over x, y_lo), lat: 8 (over z), lon: 4 (over y_hi, core).
Axes of the slice: x: 4, y: 8 (y_hi: 2, y_lo: 4; y = y_hi * 4 + y_lo), z: 8, core: 2. Of those that a mesh axis runs over, the one named last changes fastest.
Arguments:
- members_in: bfloat16 [16, 192, 384, 256], P('member', 'lat', 'lon'), may hold values from -6 to 6
- cotangent: bfloat16 [16, 192, 384, 256], P('member', 'lat', 'lon'), may hold values from -6 to 6
- spectral_filter: float32 [2, 192, 256], P(None, 'member', ('lat', 'lon')), may hold values from -6 to 6
Outputs:
- members_out: bfloat16 [16, 192, 384, 256], P('member', 'lat', 'lon')
- grads_in: bfloat16 [16, 192, 384, 256], P('member', 'lat', 'lon')
- filter_grad: float32 [2, 192, 256], P(None, 'member', ('lat', 'lon'))
The draws below stay inside these ranges and needn't reach their ends.
All inputs are finite; a program needn't handle non-finite values.
Results may differ from the reference program's by a relative error of at most 0.014.
Values may be sent and summed in bfloat16 or wider, within the bound.
A program may use at most 192 MiB of HBM per device.

```python
import math
import jax
import jax.numpy as jnp
from jax import lax

NLAT = 192
NLON = 384
MODES = 192
DEGREES = 192
CHANNELS = 256
MEMBERS = 16


def levels(own_key, dims, cuts, least, top_value):
    gain, own = 1.0, jax.random.fold_in(own_key, 6)
    for axis_at, parts in cuts:
        heights = jnp.exp(jax.random.uniform(jax.random.fold_in(own, axis_at), (parts,), jnp.float32, least / len(cuts), top_value / len(cuts)))
        gain = gain * jnp.repeat(heights, dims[axis_at] // parts).reshape([-1 if axis == axis_at else 1 for axis in range(len(dims))])
    return gain


def scatter_about(stream_key, dims, spread, most, cuts=(), held_as=jnp.bfloat16):
    loudness = levels(stream_key, dims, cuts, -0.22, 0.18) if cuts else 1.0
    array = jax.random.normal(stream_key, dims, jnp.float32) * spread * loudness
    return jnp.minimum(jnp.maximum(array, -most), most).astype(held_as)


def setup_inputs(seed: int = 0) -> dict:
    arg_keys = jax.random.split(jax.random.key(seed), 4)
    members_in = scatter_about(arg_keys[0], (MEMBERS, NLAT, NLON, CHANNELS), 1.0, 6.0, ((0, 16), (1, 8), (2, 4)))
    cotangent = scatter_about(arg_keys[1], (MEMBERS, NLAT, NLON, CHANNELS), 1.0, 6.0, ((0, 16), (1, 8), (2, 4)))
    spectral_filter = scatter_about(arg_keys[2], (2, DEGREES, CHANNELS), 1.0, 6.0, ((1, 16), (2, 32)), jnp.float32)
    return {"members_in": members_in, "cotangent": cotangent, "spectral_filter": spectral_filter}


def legendre(first_mode, mode_count, degrees, lat_count):
    colatitude = (jnp.arange(lat_count, dtype=jnp.float32) + 0.5) * (math.pi / lat_count)
    cosine = jnp.cos(colatitude)
    log_sine = jnp.log(jnp.sin(colatitude))
    orders = (first_mode + jnp.arange(mode_count, dtype=jnp.int32)).astype(jnp.float32)
    log_diag = 0.5 * jnp.log((2.0 * orders + 1.0) / (4.0 * math.pi)) + 0.5 * (lax.lgamma(orders + 0.5) - lax.lgamma(orders + 1.0) - 0.5 * math.log(math.pi))
    diagonal = jnp.exp(log_diag[:, None] + orders[:, None] * log_sine[None, :])

    def recurrence(state_pair, degree):
        earlier, latest = state_pair
        square = degree * degree - orders * orders
        upward = jnp.sqrt(jnp.maximum(4.0 * degree * degree - 1.0, 1.0) / jnp.maximum(square, 1.0))
        before = degree - 1.0
        damping = jnp.sqrt(jnp.maximum(before * before - orders * orders, 0.0) / jnp.maximum(4.0 * before * before - 1.0, 1.0))
        recurred = upward[:, None] * (cosine[None, :] * latest - damping[:, None] * earlier)
        updated = jnp.where((degree == orders)[:, None], diagonal, jnp.where((degree > orders)[:, None], recurred, 0.0))
        return ((latest, updated), updated.astype(jnp.bfloat16))
    zeros_init = jnp.zeros((mode_count, lat_count), jnp.float32)
    final_state, legendre_vals = lax.scan(recurrence, (zeros_init, zeros_init), jnp.arange(degrees, dtype=jnp.float32))
    return legendre_vals

def fourier_tables(lon_count, mode_count):
    columns = jnp.arange(lon_count, dtype=jnp.int32)
    mode_ids = jnp.arange(mode_count, dtype=jnp.int32)
    phases = (mode_ids[:, None] * columns[None, :] % lon_count).astype(jnp.float32) * (2.0 * math.pi / lon_count)
    cosines = jnp.cos(phases)
    sine_vals = jnp.sin(phases)
    factor = jnp.where(mode_ids == 0, 1.0, 2.0)[:, None]
    analysis = jnp.concatenate([cosines, -sine_vals], axis=0) * (2.0 * math.pi / lon_count)
    synthesis = jnp.concatenate([factor * cosines, -factor * sine_vals], axis=0)
    return (analysis.astype(jnp.bfloat16), synthesis.astype(jnp.bfloat16))

def quadrature(lat_count):
    colatitude = (jnp.arange(lat_count, dtype=jnp.float32) + 0.5) * (math.pi / lat_count)
    return jnp.sin(colatitude) * (math.pi / lat_count)

def apply_filter(spectral, kernel):
    kernel_real = jnp.transpose(kernel[0])[:, None, :]
    kernel_imag = jnp.transpose(kernel[1])[:, None, :]
    spec_real = spectral[:, 0]
    spec_imag = spectral[:, 1]
    return jnp.stack([kernel_real * spec_real - kernel_imag * spec_imag, kernel_real * spec_imag + kernel_imag * spec_real], axis=1)

def adjoint_filter(grads, kernel):
    kernel_real = jnp.transpose(kernel[0])[:, None, :]
    kernel_imag = jnp.transpose(kernel[1])[:, None, :]
    grad_real = grads[:, 0]
    grad_imag = grads[:, 1]
    return jnp.stack([kernel_real * grad_real + kernel_imag * grad_imag, kernel_real * grad_imag - kernel_imag * grad_real], axis=1)

def filter_terms(grads, spectral):
    grad_real = grads[:, 0]
    grad_imag = grads[:, 1]
    spec_real = spectral[:, 0]
    spec_imag = spectral[:, 1]
    first_part = lax.optimization_barrier(jnp.sum(grad_real * spec_real + grad_imag * spec_imag, axis=1))
    second_part = lax.optimization_barrier(jnp.sum(grad_imag * spec_real - grad_real * spec_imag, axis=1))
    return jnp.stack([jnp.transpose(first_part), jnp.transpose(second_part)], axis=0)

def silu_slope(values):
    sigmoid_vals = jax.nn.sigmoid(values)
    return sigmoid_vals * (1.0 + values * (1.0 - sigmoid_vals))

def reference(members_in, cotangent, spectral_filter):
    analysis, synthesis = fourier_tables(NLON, MODES)
    analysis_wide = analysis.astype(jnp.float32)
    synthesis_wide = synthesis.astype(jnp.float32)
    legendre_vals = legendre(0, MODES, DEGREES, NLAT).astype(jnp.float32)
    weights = quadrature(NLAT)

    def one_member(running, member_pair):
        state_local, grad_out = member_pair
        grid_vals = jnp.transpose(state_local, (2, 0, 1)).astype(jnp.float32)
        grad_vals = jnp.transpose(grad_out, (2, 0, 1)).astype(jnp.float32)
        fourier = (weights[None, :, None] * jnp.einsum('cjk,pk->cjp', grid_vals, analysis_wide)).astype(jnp.bfloat16)
        fourier = fourier.reshape(CHANNELS, NLAT, 2, MODES).astype(jnp.float32)
        spectral = jnp.einsum('cjrm,lmj->crml', fourier, legendre_vals)
        filtered = apply_filter(spectral, spectral_filter).astype(jnp.bfloat16).astype(jnp.float32)
        band_vals = jnp.einsum('crml,lmj->cjrm', filtered, legendre_vals).astype(jnp.bfloat16)
        band_vals = band_vals.reshape(CHANNELS, NLAT, 2 * MODES).astype(jnp.float32)
        wave_field = jnp.einsum('cjp,pk->cjk', band_vals, synthesis_wide)
        outputs = (grid_vals + jax.nn.silu(wave_field)).astype(jnp.bfloat16)
        slope_vals = (grad_vals * silu_slope(wave_field)).astype(jnp.bfloat16).astype(jnp.float32)
        grad_band = jnp.einsum('cjk,pk->cjp', slope_vals, synthesis_wide).astype(jnp.bfloat16)
        grad_band = grad_band.reshape(CHANNELS, NLAT, 2, MODES).astype(jnp.float32)
        grad_spec = jnp.einsum('cjrm,lmj->crml', grad_band, legendre_vals)
        grad_terms = filter_terms(grad_spec, spectral)
        grad_coeff = adjoint_filter(grad_spec, spectral_filter).astype(jnp.bfloat16).astype(jnp.float32)
        grad_fourier = (weights[None, :, None, None] * jnp.einsum('crml,lmj->cjrm', grad_coeff, legendre_vals)).astype(jnp.bfloat16)
        grad_fourier = grad_fourier.reshape(CHANNELS, NLAT, 2 * MODES).astype(jnp.float32)
        grads_local = (grad_vals + jnp.einsum('cjp,pk->cjk', grad_fourier, analysis_wide)).astype(jnp.bfloat16)
        return (running + grad_terms, (jnp.transpose(outputs, (1, 2, 0)), jnp.transpose(grads_local, (1, 2, 0))))
    zeros_init = jnp.zeros((2, DEGREES, CHANNELS), jnp.float32)
    running, stacked = lax.scan(one_member, zeros_init, (members_in, cotangent))
    return (stacked[0], stacked[1], running / MEMBERS)
```

```python
import functools
import math

import jax
import jax.numpy as jnp
import ml_dtypes
import numpy as np
from jax import lax
from jax.experimental import pallas as pl
from jax.experimental.pallas import tpu as pltpu
from jax.sharding import PartitionSpec as P

NLAT = 192
NLON = 384
MODES = 192
DEGREES = 192
CHANNELS = 256
MESH = pl.DeviceIdType.MESH
BF = jnp.bfloat16
F32 = jnp.float32

LATS = 8
LONS = 4
MEMBERS = 16
SITES = 16
OWN = 12
PACK = 2 * OWN
HALF = 128
COLS = NLON // LONS
CHUNKS = 3
STEP = OWN // CHUNKS
CROWS = STEP * PACK
SROWS = OWN * PACK


def fourier_constants():
    phases = (np.arange(MODES)[:, None] * np.arange(NLON)[None, :] % NLON) * (2.0 * np.pi / NLON)
    cosines, sines = np.cos(phases), np.sin(phases)
    factor = np.where(np.arange(MODES) == 0, 1.0, 2.0)[:, None]
    analysis = np.stack([cosines, -sines]) * (2.0 * np.pi / NLON)
    synthesis = np.stack([factor * cosines, -factor * sines])

    def ordered(table):
        parts = table.astype(np.float32).reshape(2, SITES, OWN, NLON)
        return parts.transpose(1, 0, 2, 3).reshape(2 * MODES, NLON).astype(ml_dtypes.bfloat16)

    analysis, synthesis = ordered(analysis), ordered(synthesis)
    return analysis, np.ascontiguousarray(analysis.T), synthesis, np.ascontiguousarray(synthesis.T)


def sphere_constants():
    theta = (np.arange(NLAT) + 0.5) * (np.pi / NLAT)
    weights = (np.sin(theta) * (np.pi / NLAT)).astype(np.float32)
    by_pair = np.repeat(weights.reshape(NLAT // 2, 2), HALF, axis=1)
    by_row = np.repeat(weights[:, None], HALF, axis=1)
    angles = np.zeros((8, 256), np.float32)
    angles[0, :NLAT] = np.cos(theta)
    angles[1, :NLAT] = np.log(np.sin(theta))
    norms = np.zeros((SITES, 16, HALF), np.float32)
    for order in range(MODES):
        log_norm = 0.5 * math.log((2.0 * order + 1.0) / (4.0 * math.pi)) + 0.5 * (
            math.lgamma(order + 0.5) - math.lgamma(order + 1.0) - 0.5 * math.log(math.pi)
        )
        norms[order // OWN, order % OWN, :] = log_norm
    return by_pair, by_row, angles, norms


def kernel(
    x_hbm, g_hbm, kf_ref, an_ref, ant_ref, sy_ref, syt_ref, wl_ref, wc_ref, ang_ref, nrm_ref,
    out_hbm, gin_hbm, fg_ref,
    xk, gk, ok, go, fs, fr, bs, br, gs, gr, hs, hr, wide, wideb, spec, leg, legt, pf,
    ksend, ka, kb, kr, k0, k1, t0, t1, ts, tr, tb, td, fin, te,
    xs, xr, cs, cr, os_, or_, ps, pr, z1s, z1r, z2s, z2r, z3s, z3r, z4s, z4r,
    kas, kar, kbs, kbr, tcs, tcr, tds, tdr, tes, ter, loc,
):
    member, lat, lon = lax.axis_index("member"), lax.axis_index("lat"), lax.axis_index("lon")
    y, q = lax.div(lon, 2), lax.rem(lon, 2)
    site = 2 * lat + q
    yoff = pl.multiple_of(HALF * y, HALF)

    def each(start, stop, body):
        def step(i, carry):
            body(i)
            return carry

        lax.fori_loop(start, stop, step, 0)

    def place(lat_to, lon_to):
        return {"lat": lat_to, "lon": lon_to}

    def site_peer(i):
        hop, dq = lax.div(i, 2), lax.rem(i, 2)
        odd = lax.rem(hop, 2)
        dz = odd * lax.div(hop + 1, 2) + (1 - odd) * (LATS - lax.div(hop, 2))
        return lax.rem(lat + dz, LATS), lax.rem(q + dq, 2)

    bar = pltpu.get_barrier_semaphore()

    def greet(i):
        to = place(lax.rem(lat + lax.div(i, LONS), LATS), lax.rem(lon + lax.rem(i, LONS), LONS))
        pl.semaphore_signal(bar, inc=1, device_id=to, device_id_type=MESH)

    def greet_member(i):
        to = {"member": lax.rem(member + i, MEMBERS)}
        pl.semaphore_signal(bar, inc=1, device_id=to, device_id_type=MESH)

    each(1, LATS * LONS, greet)
    each(1, MEMBERS, greet_member)
    pl.semaphore_wait(bar, LATS * LONS - 1 + MEMBERS - 1)

    def grid_in(src, dst, ssem, rsem, ch, i):
        lon_to = lax.rem(lon + i, LONS)
        y_to, q_to = lax.div(lon_to, 2), lax.rem(lon_to, 2)
        part = src.at[
            pl.ds(OWN * q_to + STEP * ch, STEP), :, pl.ds(pl.multiple_of(HALF * y_to, HALF), HALF)
        ]
        rows = pl.ds(pl.multiple_of(COLS * lon, COLS), COLS)
        return pltpu.make_async_remote_copy(
            src_ref=part, dst_ref=dst.at[pl.ds(STEP * ch, STEP), rows, :],
            send_sem=ssem.at[ch, i], recv_sem=rsem.at[ch, i],
            device_id=place(lat, lon_to), device_id_type=MESH,
        )

    def grid_in_own(src, dst, sem, ch):
        rows = pl.ds(pl.multiple_of(COLS * lon, COLS), COLS)
        return pltpu.make_async_copy(
            src.at[pl.ds(OWN * q + STEP * ch, STEP), :, pl.ds(yoff, HALF)],
            dst.at[pl.ds(STEP * ch, STEP), rows, :],
            sem.at[ch, 0],
        )

    def grid_out(src, dst, ssem, rsem, ch, i):
        lon_to = lax.rem(lon + i, LONS)
        rows = pl.ds(pl.multiple_of(COLS * lon_to, COLS), COLS)
        return pltpu.make_async_remote_copy(
            src_ref=src.at[pl.ds(STEP * ch, STEP), rows, :],
            dst_ref=dst.at[pl.ds(OWN * q + STEP * ch, STEP), :, pl.ds(yoff, HALF)],
            send_sem=ssem.at[ch, i], recv_sem=rsem.at[ch, i],
            device_id=place(lat, lon_to), device_id_type=MESH,
        )

    def grid_out_own(src, dst, sem, ch):
        rows = pl.ds(pl.multiple_of(COLS * lon, COLS), COLS)
        return pltpu.make_async_copy(
            src.at[pl.ds(STEP * ch, STEP), rows, :],
            dst.at[pl.ds(OWN * q + STEP * ch, STEP), :, pl.ds(yoff, HALF)],
            sem.at[ch, 0],
        )

    def site_copy(src, dst, ssem, rsem, ch, i):
        lat_to, q_to = site_peer(i)
        rows = pl.ds(CROWS * ch, CROWS)
        return pltpu.make_async_remote_copy(
            src_ref=src.at[2 * lat_to + q_to, rows, :], dst_ref=dst.at[site, rows, :],
            send_sem=ssem.at[ch, i], recv_sem=rsem.at[ch, i],
            device_id=place(lat_to, 2 * y + q_to), device_id_type=MESH,
        )

    def site_own(src, dst, sem, ch):
        rows = pl.ds(CROWS * ch, CROWS)
        return pltpu.make_async_copy(src.at[site, rows, :], dst.at[site, rows, :], sem.at[ch, 0])

    def send_grid(src, dst, ssem, rsem, ch, own, remote):
        each(1, LONS, lambda i: remote(src, dst, ssem, rsem, ch, i).start())
        own(src, dst, rsem, ch).start()

    def take_grid(src, dst, ssem, rsem, ch, own, remote):
        each(1, LONS, lambda i: remote(src, dst, ssem, rsem, ch, i).wait_recv())
        own(src, dst, rsem, ch).wait()

    def send_site(src, dst, ssem, rsem, ch):
        each(1, SITES, lambda i: site_copy(src, dst, ssem, rsem, ch, i).start())
        site_own(src, dst, rsem, ch).start()

    def take_site(src, dst, ssem, rsem, ch):
        each(1, SITES, lambda i: site_copy(src, dst, ssem, rsem, ch, i).wait_recv())
        site_own(src, dst, rsem, ch).wait()

    for ch in range(CHUNKS):
        send_grid(x_hbm, xk, xs, xr, ch, grid_in_own, grid_in)

    lanes = lax.broadcasted_iota(jnp.int32, (OWN, HALF), 1)
    y_own = lax.div(lat, LATS // 2)
    slot = lax.rem(lat, LATS // 2) * LONS + lon
    inside = lax.div(lanes, 8) == slot
    for part in range(2):
        values = kf_ref[part]
        spread = jnp.zeros((OWN, HALF), F32)
        for col in range(8):
            spread = jnp.where(lax.rem(lanes, 8) == col, values[:, col : col + 1], spread)
        ksend[pl.ds(part * OWN, OWN), :] = jnp.where(inside, spread, 0.0)

    def owner_copy(i):
        site_to = lax.rem(site + i, SITES)
        lat_to, q_to = lax.div(site_to, 2), lax.rem(site_to, 2)
        return pltpu.make_async_remote_copy(
            src_ref=ksend, dst_ref=ka.at[slot], send_sem=kas.at[i], recv_sem=kar.at[slot],
            device_id=place(lat_to, 2 * y_own + q_to), device_id_type=MESH,
        )

    each(1, SITES, lambda i: owner_copy(i).start())

    @pl.when(y_own == y)
    def _():
        ka[slot] = ksend[...]

    @pl.when(y_own != y)
    def _():
        owner_copy(0).start()

    orders = (OWN * site + lax.broadcasted_iota(jnp.int32, (16, HALF), 0)).astype(F32)
    squares = orders * orders
    cosine = [ang_ref[pl.ds(0, 1), pl.ds(HALF * h, HALF)] for h in range(2)]
    logsin = [ang_ref[pl.ds(1, 1), pl.ds(HALF * h, HALF)] for h in range(2)]
    diagonal = [jnp.exp(nrm_ref[site] + orders * logsin[h]) for h in range(2)]

    def degree_step(l, carry):
        degree = jnp.full((16, HALF), l, jnp.int32).astype(F32)
        before = degree - 1.0
        upward = jnp.sqrt(
            jnp.maximum(4.0 * degree * degree - 1.0, 1.0)
            / jnp.maximum(degree * degree - squares, 1.0)
        )
        damping = jnp.sqrt(
            jnp.maximum(before * before - squares, 0.0)
            / jnp.maximum(4.0 * before * before - 1.0, 1.0)
        )
        state = []
        for h in range(2):
            earlier, latest = carry[2 * h], carry[2 * h + 1]
            recurred = upward * (cosine[h] * latest - damping * earlier)
            updated = jnp.where(
                degree == orders, diagonal[h], jnp.where(degree > orders, recurred, 0.0)
            )
            pf[h, pl.ds(pl.multiple_of(16 * l, 16), 16), :] = updated
            state += [latest, updated]
        return tuple(state)

    start = tuple(diagonal[h] * 0.0 for h in (0, 0, 1, 1))
    lax.fori_loop(0, DEGREES, degree_step, start, unroll=4)
    for m in range(OWN):
        table = jnp.concatenate(
            [pf[h, pl.ds(m, DEGREES, stride=16), :] for h in range(2)], axis=1
        )
        leg[m] = table[:, :NLAT].astype(BF)
        legt[m] = jnp.transpose(table)[:NLAT].astype(BF)

    def pack_pair(values, ref, pair):
        rows = pl.ds(pl.multiple_of(2 * PACK * pair, 2 * PACK), 2 * PACK)
        for d in range(SITES):
            block = values[PACK * d : PACK * (d + 1)]
            ref[d, rows, :] = jnp.concatenate([block[:, :HALF], block[:, HALF:]], axis=0).astype(BF)

    def unpack_pair(ref, pair):
        rows = pl.ds(pl.multiple_of(2 * PACK * pair, 2 * PACK), 2 * PACK)
        blocks = [ref[d, rows, :].astype(F32) for d in range(SITES)]
        first = jnp.concatenate([block[:PACK] for block in blocks], axis=0).astype(BF)
        second = jnp.concatenate([block[PACK:] for block in blocks], axis=0).astype(BF)
        return jnp.concatenate([first, second], axis=1)

    def dot(a, b):
        return jnp.dot(a, b, preferred_element_type=F32)

    def pairs_of(ch, body):
        each(ch * (STEP // 2), (ch + 1) * (STEP // 2), body)

    def analyse(pair):
        field = jnp.concatenate([xk[2 * pair], xk[2 * pair + 1]], axis=1)
        weight = wl_ref[pl.ds((OWN // 2) * site + pair, 1), :]
        pack_pair(dot(an_ref[...], field) * weight, fs, pair)

    for ch in range(CHUNKS):
        take_grid(x_hbm, xk, xs, xr, ch, grid_in_own, grid_in)
        pairs_of(ch, analyse)
        send_site(fs, fr, z1s, z1r, ch)
    for ch in range(CHUNKS):
        send_grid(g_hbm, gk, cs, cr, ch, grid_in_own, grid_in)

    def owner_wait(o):
        @pl.when(jnp.logical_or(y_own != y, o != slot))
        def _():
            pltpu.make_async_remote_copy(
                src_ref=ksend, dst_ref=ka.at[o], send_sem=kas.at[0], recv_sem=kar.at[o],
                device_id=place(lat, lon), device_id_type=MESH,
            ).wait_recv()

    each(0, SITES, owner_wait)
    kb[...] = jnp.sum(ka[...], axis=0)

    def member_copy(i):
        return pltpu.make_async_remote_copy(
            src_ref=kb, dst_ref=kr.at[member], send_sem=kbs.at[i], recv_sem=kbr.at[i],
            device_id={"member": lax.rem(member + i, MEMBERS)}, device_id_type=MESH,
        )

    each(1, MEMBERS, lambda i: member_copy(i).start())
    kr[member] = kb[...]
    each(1, MEMBERS, lambda i: member_copy(i).wait_recv())
    for block in range(MEMBERS):
        k0[pl.ds(OWN * block, OWN), :] = kr[block, pl.ds(0, OWN), :]
        k1[pl.ds(OWN * block, OWN), :] = kr[block, pl.ds(OWN, OWN), :]

    def widen(ref):
        for d in range(SITES):
            wide[pl.ds(SROWS * d, SROWS), :] = ref[d].astype(F32)

    def narrow(ref):
        for d in range(SITES):
            ref[d] = wideb[pl.ds(SROWS * d, SROWS), :].astype(BF)

    def mode_in(m):
        return jnp.concatenate(
            [wide[pl.ds(part * OWN + m, NLAT, stride=PACK), :] for part in range(2)], axis=1
        ).astype(BF)

    def mode_out(m, values):
        for part in range(2):
            wideb[pl.ds(part * OWN + m, NLAT, stride=PACK), :] = values[
                :, HALF * part : HALF * (part + 1)
            ]

    for ch in range(CHUNKS):
        take_site(fs, fr, z1s, z1r, ch)
    widen(fr)
    for m in range(OWN):
        spectral = dot(leg[m], mode_in(m))
        spec[m] = spectral
        real, imag = spectral[:, :HALF], spectral[:, HALF:]
        filtered = jnp.concatenate(
            [k0[...] * real - k1[...] * imag, k0[...] * imag + k1[...] * real], axis=1
        ).astype(BF)
        mode_out(m, dot(legt[m], filtered))
    narrow(bs)
    for ch in range(CHUNKS):
        send_site(bs, br, z2s, z2r, ch)

    def grid_stage(pair):
        wave = dot(syt_ref[...], unpack_pair(br, pair))
        slopes = []
        for side in range(2):
            value = wave[:, HALF * side : HALF * (side + 1)]
            sig = jax.nn.sigmoid(value)
            j = 2 * pair + side
            ok[j] = (xk[j].astype(F32) + value * sig).astype(BF)
            slope = gk[j].astype(F32) * (sig * (1.0 + value * (1.0 - sig)))
            slopes.append(slope.astype(BF))
        pack_pair(dot(sy_ref[...], jnp.concatenate(slopes, axis=1)), gs, pair)

    for ch in range(CHUNKS):
        take_grid(g_hbm, gk, cs, cr, ch, grid_in_own, grid_in)
    for ch in range(CHUNKS):
        take_site(bs, br, z2s, z2r, ch)
        pairs_of(ch, grid_stage)
        send_site(gs, gr, z3s, z3r, ch)
        send_grid(ok, out_hbm, os_, or_, ch, grid_out_own, grid_out)

    for ch in range(CHUNKS):
        take_site(gs, gr, z3s, z3r, ch)
    widen(gr)
    t0[...] = jnp.zeros_like(t0)
    t1[...] = jnp.zeros_like(t1)
    weights = jnp.concatenate([wc_ref[...], wc_ref[...]], axis=1)
    for m in range(OWN):
        grad = dot(leg[m], mode_in(m))
        spectral = spec[m]
        real, imag = spectral[:, :HALF], spectral[:, HALF:]
        greal, gimag = grad[:, :HALF], grad[:, HALF:]
        t0[...] += greal * real + gimag * imag
        t1[...] += gimag * real - greal * imag
        coeff = jnp.concatenate(
            [k0[...] * greal + k1[...] * gimag, k0[...] * gimag - k1[...] * greal], axis=1
        ).astype(BF)
        mode_out(m, dot(legt[m], coeff) * weights)
    narrow(hs)
    for ch in range(CHUNKS):
        send_site(hs, hr, z4s, z4r, ch)

    for block in range(SITES):
        ts[block, pl.ds(0, OWN), :] = t0[pl.ds(OWN * block, OWN), :]
        ts[block, pl.ds(OWN, OWN), :] = t1[pl.ds(OWN * block, OWN), :]

    def terms_copy(i):
        lat_to, q_to = site_peer(i)
        return pltpu.make_async_remote_copy(
            src_ref=ts.at[2 * lat_to + q_to], dst_ref=tr.at[site],
            send_sem=tcs.at[i], recv_sem=tcr.at[i],
            device_id=place(lat_to, 2 * y + q_to), device_id_type=MESH,
        )

    each(1, SITES, lambda i: terms_copy(i).start())
    tr[site] = ts[site]

    def degree_copy():
        return pltpu.make_async_remote_copy(
            src_ref=tb, dst_ref=td.at[member], send_sem=tds.at[0], recv_sem=tdr.at[member],
            device_id={"member": site}, device_id_type=MESH,
        )

    def channel_copy(i):
        lat_to, lon_to = (LATS // 2) * y + lax.div(i, LONS), lax.rem(i, LONS)
        return pltpu.make_async_remote_copy(
            src_ref=fin, dst_ref=te, send_sem=tes.at[i], recv_sem=ter.at[0],
            device_id=place(lat_to, lon_to), device_id_type=MESH,
        )

    def is_self(i):
        return jnp.logical_and(
            (LATS // 2) * y + lax.div(i, LONS) == lat, lax.rem(i, LONS) == lon
        )

    def terms_to_member():
        each(1, SITES, lambda i: terms_copy(i).wait_recv())
        tb[...] = jnp.sum(tr[...], axis=0)

        @pl.when(member != site)
        def _():
            degree_copy().start()

        @pl.when(member == site)
        def _():
            td[member] = tb[...]

    def terms_to_owner():
        @pl.when(member == site)
        def _():
            def arrive(o):
                @pl.when(o != member)
                def _():
                    pltpu.make_async_remote_copy(
                        src_ref=tb, dst_ref=td.at[o], send_sem=tds.at[0], recv_sem=tdr.at[o],
                        device_id=place(lat, lon), device_id_type=MESH,
                    ).wait_recv()

            each(0, MEMBERS, arrive)
            fin[...] = jnp.sum(td[...], axis=0) * (1.0 / MEMBERS)

            def spread(i):
                @pl.when(jnp.logical_not(is_self(i)))
                def _():
                    channel_copy(i).start()

                @pl.when(is_self(i))
                def _():
                    te[...] = fin[...]

            each(0, SITES, spread)

    reducer_is_self = jnp.logical_and(
        lax.div(member, 2) == lat, 2 * y_own + lax.rem(member, 2) == lon
    )

    def terms_finish():
        @pl.when(jnp.logical_not(reducer_is_self))
        def _():
            channel_copy(0).wait_recv()

        cols = lax.broadcasted_iota(jnp.int32, (OWN, 8), 1)
        for part in range(2):
            block = te[pl.ds(part * OWN, OWN), :]
            result = jnp.zeros((OWN, 8), F32)
            for col in range(8):
                one = jnp.sum(
                    jnp.where(lanes == 8 * slot + col, block, 0.0), axis=1, keepdims=True
                )
                result = jnp.where(cols == col, one, result)
            fg_ref[part] = result

    def last_stage(pair):
        field = dot(ant_ref[...], unpack_pair(hr, pair))
        for side in range(2):
            j = 2 * pair + side
            go[j] = (gk[j].astype(F32) + field[:, HALF * side : HALF * (side + 1)]).astype(BF)

    for ch in range(CHUNKS):
        take_site(hs, hr, z4s, z4r, ch)
        pairs_of(ch, last_stage)
        send_grid(go, gin_hbm, ps, pr, ch, grid_out_own, grid_out)
        if ch == 0:
            terms_to_member()
        if ch == 1:
            terms_to_owner()
    terms_finish()

    for ch in range(CHUNKS):
        take_grid(ok, out_hbm, os_, or_, ch, grid_out_own, grid_out)
        take_grid(go, gin_hbm, ps, pr, ch, grid_out_own, grid_out)

    for ch in range(CHUNKS):
        each(1, LONS, lambda i: grid_in(x_hbm, xk, xs, xr, ch, i).wait_send())
        each(1, LONS, lambda i: grid_in(g_hbm, gk, cs, cr, ch, i).wait_send())
        each(1, LONS, lambda i: grid_out(ok, out_hbm, os_, or_, ch, i).wait_send())
        each(1, LONS, lambda i: grid_out(go, gin_hbm, ps, pr, ch, i).wait_send())
        each(1, SITES, lambda i: site_copy(fs, fr, z1s, z1r, ch, i).wait_send())
        each(1, SITES, lambda i: site_copy(bs, br, z2s, z2r, ch, i).wait_send())
        each(1, SITES, lambda i: site_copy(gs, gr, z3s, z3r, ch, i).wait_send())
        each(1, SITES, lambda i: site_copy(hs, hr, z4s, z4r, ch, i).wait_send())
    each(1, SITES, lambda i: owner_copy(i).wait_send())

    @pl.when(y_own != y)
    def _():
        owner_copy(0).wait_send()

    each(1, MEMBERS, lambda i: member_copy(i).wait_send())
    each(1, SITES, lambda i: terms_copy(i).wait_send())

    @pl.when(member != site)
    def _():
        degree_copy().wait_send()

    @pl.when(member == site)
    def _():
        def left(i):
            @pl.when(jnp.logical_not(is_self(i)))
            def _():
                channel_copy(i).wait_send()

        each(0, SITES, left)


def on_device(members_in, cotangent, spectral_filter):
    vmem = pl.BlockSpec(memory_space=pltpu.VMEM)
    anywhere = pl.BlockSpec(memory_space=pl.ANY)
    block = members_in.shape[1:]
    grid_buf = pltpu.VMEM((OWN, NLON, HALF), BF)
    site_buf = pltpu.VMEM((SITES, SROWS, HALF), BF)
    small = pltpu.VMEM((PACK, HALF), F32)
    many = pltpu.VMEM((SITES, PACK, HALF), F32)
    plane = pltpu.VMEM((DEGREES, HALF), F32)
    flat = pltpu.VMEM((SITES * SROWS, HALF), F32)
    table = pltpu.VMEM((OWN, DEGREES, NLAT), BF)
    grid_sem = pltpu.SemaphoreType.DMA((CHUNKS, LONS))
    site_sem = pltpu.SemaphoreType.DMA((CHUNKS, SITES))
    many_sem = pltpu.SemaphoreType.DMA((SITES,))
    one_sem = pltpu.SemaphoreType.DMA((1,))
    scratch = (
        [grid_buf] * 4
        + [site_buf] * 8
        + [flat] * 2
        + [pltpu.VMEM((OWN, DEGREES, 2 * HALF), F32)]
        + [table] * 2
        + [pltpu.VMEM((2, DEGREES * 16, HALF), F32)]
        + [small, many, small, many]
        + [plane] * 4
        + [many, many, small, many, small, small]
        + [grid_sem] * 8
        + [site_sem] * 8
        + [many_sem] * 6
        + [one_sem, many_sem, many_sem, one_sem, one_sem]
    )
    outputs, grads, filter_grad = pl.pallas_call(
        kernel,
        out_shape=(
            jax.ShapeDtypeStruct(block, BF),
            jax.ShapeDtypeStruct(block, BF),
            jax.ShapeDtypeStruct(spectral_filter.shape, F32),
        ),
        in_specs=[anywhere, anywhere] + [vmem] * 9,
        out_specs=(anywhere, anywhere, vmem),
        scratch_shapes=scratch,
        compiler_params=pltpu.CompilerParams(
            collective_id=0, has_side_effects=True, vmem_limit_bytes=56 * 1024 * 1024
        ),
        name="sphere",
    )(
        members_in[0], cotangent[0], spectral_filter, *fourier_constants(), *sphere_constants()
    )
    return outputs[None], grads[None], filter_grad


def solution(mesh):
    placed = (
        P("member", "lat", "lon", None),
        P("member", "lat", "lon", None),
        P(None, "member", ("lat", "lon")),
    )
    return jax.shard_map(
        on_device, mesh=mesh, in_specs=placed, out_specs=placed, check_vma=False
    )
```

```python
import functools
import math

import jax
import jax.numpy as jnp
import ml_dtypes
import numpy as np
from jax import lax
from jax.experimental import pallas as pl
from jax.experimental.pallas import tpu as pltpu
from jax.sharding import PartitionSpec as P

NLAT = 192
NLON = 384
MODES = 192
DEGREES = 192
CHANNELS = 256
MESH = pl.DeviceIdType.MESH
BF = jnp.bfloat16
F32 = jnp.float32

LATS = 8
LONS = 4
MEMBERS = 16
SITES = 16
OWN = 12
PACK = 2 * OWN
HALF = 128
COLS = NLON // LONS
CHUNKS = 6
KMIX = 1
STEP = OWN // CHUNKS
CROWS = STEP * PACK
SROWS = OWN * PACK


def fourier_constants():
    phases = (np.arange(MODES)[:, None] * np.arange(NLON)[None, :] % NLON) * (2.0 * np.pi / NLON)
    cosines, sines = np.cos(phases), np.sin(phases)
    factor = np.where(np.arange(MODES) == 0, 1.0, 2.0)[:, None]
    analysis = np.stack([cosines, -sines]) * (2.0 * np.pi / NLON)
    synthesis = np.stack([factor * cosines, -factor * sines])

    def ordered(table):
        parts = table.astype(np.float32).reshape(2, SITES, OWN, NLON)
        return parts.transpose(1, 0, 2, 3).reshape(2 * MODES, NLON).astype(ml_dtypes.bfloat16)

    analysis, synthesis = ordered(analysis), ordered(synthesis)
    return analysis, np.ascontiguousarray(analysis.T), synthesis, np.ascontiguousarray(synthesis.T)


def sphere_constants():
    theta = (np.arange(NLAT) + 0.5) * (np.pi / NLAT)
    weights = (np.sin(theta) * (np.pi / NLAT)).astype(np.float32)
    by_pair = np.repeat(weights.reshape(NLAT // 2, 2), HALF, axis=1)
    by_row = np.repeat(weights[:, None], HALF, axis=1)
    angles = np.zeros((8, 256), np.float32)
    angles[0, :NLAT] = np.cos(theta)
    angles[1, :NLAT] = np.log(np.sin(theta))
    norms = np.zeros((SITES, 16, HALF), np.float32)
    for order in range(MODES):
        log_norm = 0.5 * math.log((2.0 * order + 1.0) / (4.0 * math.pi)) + 0.5 * (
            math.lgamma(order + 0.5) - math.lgamma(order + 1.0) - 0.5 * math.log(math.pi)
        )
        norms[order // OWN, order % OWN, :] = log_norm
    return by_pair, by_row, angles, norms


def kernel(
    x_hbm, g_hbm, kf_ref, an_ref, ant_ref, sy_ref, syt_ref, wl_ref, wc_ref, ang_ref, nrm_ref,
    out_hbm, gin_hbm, fg_ref,
    xk, gk, ok, go, fs, fr, bs, br, gs, gr, hs, hr, wide, wideb, spec, leg, legt, pf,
    ksend, ka, kb, kr, k0, k1, t0, t1, ts, tp, tq, tr, tb, td, fin, te,
    xs, xr, cs, cr, os_, or_, ps, pr, z1s, z1r, z2s, z2r, z3s, z3r, z4s, z4r,
    kas, kar, kbs, kbr, tcs, tcr, tds, tdr, tes, ter, tps, tpr, kcs, kcr,
):
    member, lat, lon = lax.axis_index("member"), lax.axis_index("lat"), lax.axis_index("lon")
    y, q = lax.div(lon, 2), lax.rem(lon, 2)
    site = 2 * lat + q
    yoff = pl.multiple_of(HALF * y, HALF)

    def each(start, stop, body):
        def step(i, carry):
            body(i)
            return carry

        lax.fori_loop(start, stop, step, 0)

    def place(lat_to, lon_to):
        return {"lat": lat_to, "lon": lon_to}

    def site_peer(i):
        hop, dq = lax.div(i, 2), lax.rem(i, 2)
        odd = lax.rem(hop, 2)
        dz = odd * lax.div(hop + 1, 2) + (1 - odd) * (LATS - lax.div(hop, 2))
        return lax.rem(lat + dz, LATS), lax.rem(q + dq, 2)

    bar = pltpu.get_barrier_semaphore()

    def greet(i):
        to = place(lax.rem(lat + lax.div(i, LONS), LATS), lax.rem(lon + lax.rem(i, LONS), LONS))
        pl.semaphore_signal(bar, inc=1, device_id=to, device_id_type=MESH)

    def greet_member(i):
        to = {"member": lax.rem(member + i, MEMBERS)}
        pl.semaphore_signal(bar, inc=1, device_id=to, device_id_type=MESH)

    each(1, LATS * LONS, greet)
    each(1, MEMBERS, greet_member)
    pl.semaphore_wait(bar, LATS * LONS - 1 + MEMBERS - 1)

    def grid_in(src, dst, ssem, rsem, ch, i):
        lon_to = lax.rem(lon + i, LONS)
        y_to, q_to = lax.div(lon_to, 2), lax.rem(lon_to, 2)
        part = src.at[
            pl.ds(OWN * q_to + STEP * ch, STEP), :, pl.ds(pl.multiple_of(HALF * y_to, HALF), HALF)
        ]
        rows = pl.ds(pl.multiple_of(COLS * lon, COLS), COLS)
        return pltpu.make_async_remote_copy(
            src_ref=part, dst_ref=dst.at[pl.ds(STEP * ch, STEP), rows, :],
            send_sem=ssem.at[ch, i], recv_sem=rsem.at[ch, i],
            device_id=place(lat, lon_to), device_id_type=MESH,
        )

    def grid_in_own(src, dst, sem, ch):
        rows = pl.ds(pl.multiple_of(COLS * lon, COLS), COLS)
        return pltpu.make_async_copy(
            src.at[pl.ds(OWN * q + STEP * ch, STEP), :, pl.ds(yoff, HALF)],
            dst.at[pl.ds(STEP * ch, STEP), rows, :],
            sem.at[ch, 0],
        )

    def grid_out(src, dst, ssem, rsem, ch, i):
        lon_to = lax.rem(lon + i, LONS)
        rows = pl.ds(pl.multiple_of(COLS * lon_to, COLS), COLS)
        return pltpu.make_async_remote_copy(
            src_ref=src.at[pl.ds(STEP * ch, STEP), rows, :],
            dst_ref=dst.at[pl.ds(OWN * q + STEP * ch, STEP), :, pl.ds(yoff, HALF)],
            send_sem=ssem.at[ch, i], recv_sem=rsem.at[ch, i],
            device_id=place(lat, lon_to), device_id_type=MESH,
        )

    def grid_out_own(src, dst, sem, ch):
        rows = pl.ds(pl.multiple_of(COLS * lon, COLS), COLS)
        return pltpu.make_async_copy(
            src.at[pl.ds(STEP * ch, STEP), rows, :],
            dst.at[pl.ds(OWN * q + STEP * ch, STEP), :, pl.ds(yoff, HALF)],
            sem.at[ch, 0],
        )

    def site_copy(src, dst, ssem, rsem, ch, i):
        lat_to, q_to = site_peer(i)
        rows = pl.ds(CROWS * ch, CROWS)
        return pltpu.make_async_remote_copy(
            src_ref=src.at[2 * lat_to + q_to, rows, :], dst_ref=dst.at[site, rows, :],
            send_sem=ssem.at[ch, i], recv_sem=rsem.at[ch, i],
            device_id=place(lat_to, 2 * y + q_to), device_id_type=MESH,
        )

    def site_own(src, dst, sem, ch):
        rows = pl.ds(CROWS * ch, CROWS)
        return pltpu.make_async_copy(src.at[site, rows, :], dst.at[site, rows, :], sem.at[ch, 0])

    def send_grid(src, dst, ssem, rsem, ch, own, remote):
        each(1, LONS, lambda i: remote(src, dst, ssem, rsem, ch, i).start())
        own(src, dst, rsem, ch).start()

    def take_grid(src, dst, ssem, rsem, ch, own, remote):
        each(1, LONS, lambda i: remote(src, dst, ssem, rsem, ch, i).wait_recv())
        own(src, dst, rsem, ch).wait()

    def send_site(src, dst, ssem, rsem, ch):
        each(1, SITES, lambda i: site_copy(src, dst, ssem, rsem, ch, i).start())
        site_own(src, dst, rsem, ch).start()

    def take_site(src, dst, ssem, rsem, ch):
        each(1, SITES, lambda i: site_copy(src, dst, ssem, rsem, ch, i).wait_recv())
        site_own(src, dst, rsem, ch).wait()

    y_own = lax.div(lat, LATS // 2)
    slot = lax.rem(lat, LATS // 2) * LONS + lon
    def exact(a, b, dims):
        return lax.dot_general(
            a, b, (dims, ((), ())), precision=lax.Precision.HIGHEST, preferred_element_type=F32
        )

    def iota(shape, dim):
        return lax.broadcasted_iota(jnp.int32, shape, dim)

    degree_rows = (lax.div(iota((OWN, HALF), 1), 8) == iota((OWN, HALF), 0)).astype(F32)
    channel_rows = lax.rem(iota((8, HALF), 1), 8) == iota((8, HALF), 0)
    for part in range(2):
        spread = exact(kf_ref[part], degree_rows, ((1,), (0,)))
        ksend[pl.ds(part, 1), :] = jnp.sum(
            jnp.where(channel_rows, spread, 0.0), axis=0, keepdims=True
        )
    select = (iota((8, HALF), 1) == 8 * slot + iota((8, HALF), 0)).astype(F32)

    collects = member == site
    collector_is_self = jnp.logical_and(
        lax.div(member, 2) == lat, 2 * y_own + lax.rem(member, 2) == lon
    )

    def owner_copy():
        return pltpu.make_async_remote_copy(
            src_ref=ksend, dst_ref=ka.at[slot], send_sem=kas.at[0], recv_sem=kar.at[slot],
            device_id=place(lax.div(member, 2), 2 * y_own + lax.rem(member, 2)),
            device_id_type=MESH,
        )

    @pl.when(collector_is_self)
    def _():
        ka[slot] = ksend[...]

    @pl.when(jnp.logical_not(collector_is_self))
    def _():
        owner_copy().start()

    for ch in range(2):
        send_grid(x_hbm, xk, xs, xr, ch, grid_in_own, grid_in)

    def owner_wait(o):
        @pl.when(jnp.logical_or(y_own != y, o != slot))
        def _():
            pltpu.make_async_remote_copy(
                src_ref=ksend, dst_ref=ka.at[o], send_sem=kas.at[0], recv_sem=kar.at[o],
                device_id=place(lat, lon), device_id_type=MESH,
            ).wait_recv()

    def member_copy(i):
        return pltpu.make_async_remote_copy(
            src_ref=kb, dst_ref=kr.at[member], send_sem=kbs.at[i], recv_sem=kbr.at[0],
            device_id={"member": lax.rem(member + i, MEMBERS)}, device_id_type=MESH,
        )

    def degrees_copy(i):
        lat_to, q_to = site_peer(i)
        return pltpu.make_async_remote_copy(
            src_ref=kr.at[site], dst_ref=kr.at[site], send_sem=kcs.at[i], recv_sem=kcr.at[i],
            device_id=place(lat_to, 2 * y + q_to), device_id_type=MESH,
        )

    @pl.when(collects)
    def _():
        each(0, SITES, owner_wait)
        owner_rows = (lax.div(iota((HALF, SITES), 0), 8) == iota((HALF, SITES), 1)).astype(F32)
        own_lanes = lax.rem(iota((HALF, HALF), 1), 8) == lax.rem(iota((HALF, HALF), 0), 8)
        for part in range(2):
            rows = jnp.concatenate([ka[o, pl.ds(part, 1), :] for o in range(SITES)], axis=0)
            spread = jnp.where(own_lanes, exact(owner_rows, rows, ((1,), (0,))), 0.0)
            kb[pl.ds(part * OWN, OWN), :] = exact(degree_rows, spread, ((1,), (1,)))
        each(1, MEMBERS, lambda i: member_copy(i).start())
        kr[member] = kb[...]

    def degrees_to_sites():
        @pl.when(jnp.logical_not(collects))
        def _():
            member_copy(1).wait_recv()

        each(1, SITES, lambda i: degrees_copy(i).start())

    for ch in range(2, CHUNKS):
        send_grid(x_hbm, xk, xs, xr, ch, grid_in_own, grid_in)

    orders = (OWN * site + lax.broadcasted_iota(jnp.int32, (16, HALF), 0)).astype(F32)
    squares = orders * orders
    cosine = [ang_ref[pl.ds(0, 1), pl.ds(HALF * h, HALF)] for h in range(2)]
    logsin = [ang_ref[pl.ds(1, 1), pl.ds(HALF * h, HALF)] for h in range(2)]
    diagonal = [jnp.exp(nrm_ref[site] + orders * logsin[h]) for h in range(2)]

    def degree_step(l, carry):
        degree = jnp.full((16, HALF), l, jnp.int32).astype(F32)
        before = degree - 1.0
        upward = jnp.sqrt(
            jnp.maximum(4.0 * degree * degree - 1.0, 1.0)
            / jnp.maximum(degree * degree - squares, 1.0)
        )
        damping = jnp.sqrt(
            jnp.maximum(before * before - squares, 0.0)
            / jnp.maximum(4.0 * before * before - 1.0, 1.0)
        )
        state = []
        for h in range(2):
            earlier, latest = carry[2 * h], carry[2 * h + 1]
            recurred = upward * (cosine[h] * latest - damping * earlier)
            updated = jnp.where(
                degree == orders, diagonal[h], jnp.where(degree > orders, recurred, 0.0)
            )
            pf[h, pl.ds(pl.multiple_of(16 * l, 16), 16), :] = updated
            state += [latest, updated]
        return tuple(state)

    start = tuple(diagonal[h] * 0.0 for h in (0, 0, 1, 1))
    lax.fori_loop(0, DEGREES, degree_step, start, unroll=4)
    for m in range(OWN):
        table = jnp.concatenate(
            [pf[h, pl.ds(m, DEGREES, stride=16), :] for h in range(2)], axis=1
        )
        leg[m] = table[:, :NLAT].astype(BF)
        legt[m] = jnp.transpose(table)[:NLAT].astype(BF)

    def pack_pair(values, ref, pair):
        rows = pl.ds(pl.multiple_of(2 * PACK * pair, 2 * PACK), 2 * PACK)
        for d in range(SITES):
            block = values[PACK * d : PACK * (d + 1)]
            ref[d, rows, :] = jnp.concatenate([block[:, :HALF], block[:, HALF:]], axis=0).astype(BF)

    def unpack_pair(ref, pair):
        rows = pl.ds(pl.multiple_of(2 * PACK * pair, 2 * PACK), 2 * PACK)
        blocks = [ref[d, rows, :].astype(F32) for d in range(SITES)]
        first = jnp.concatenate([block[:PACK] for block in blocks], axis=0).astype(BF)
        second = jnp.concatenate([block[PACK:] for block in blocks], axis=0).astype(BF)
        return jnp.concatenate([first, second], axis=1)

    def dot(a, b):
        return jnp.dot(a, b, preferred_element_type=F32)

    def pairs_of(ch, body):
        each(ch * (STEP // 2), (ch + 1) * (STEP // 2), body)

    def analyse(pair):
        field = jnp.concatenate([xk[2 * pair], xk[2 * pair + 1]], axis=1)
        weight = wl_ref[pl.ds((OWN // 2) * site + pair, 1), :]
        pack_pair(dot(an_ref[...], field) * weight, fs, pair)

    for ch in range(CHUNKS):
        take_grid(x_hbm, xk, xs, xr, ch, grid_in_own, grid_in)
        pairs_of(ch, analyse)
        send_site(fs, fr, z1s, z1r, ch)
        if ch == KMIX:
            degrees_to_sites()
    for ch in range(CHUNKS):
        send_grid(g_hbm, gk, cs, cr, ch, grid_in_own, grid_in)

    def widen(ref):
        for d in range(SITES):
            wide[pl.ds(SROWS * d, SROWS), :] = ref[d].astype(F32)

    def narrow(ref):
        for d in range(SITES):
            ref[d] = wideb[pl.ds(SROWS * d, SROWS), :].astype(BF)

    def mode_in(m):
        return jnp.concatenate(
            [wide[pl.ds(part * OWN + m, NLAT, stride=PACK), :] for part in range(2)], axis=1
        ).astype(BF)

    def mode_out(m, values):
        for part in range(2):
            wideb[pl.ds(part * OWN + m, NLAT, stride=PACK), :] = values[
                :, HALF * part : HALF * (part + 1)
            ]

    for ch in range(CHUNKS):
        take_site(fs, fr, z1s, z1r, ch)
    each(1, SITES, lambda i: degrees_copy(i).wait_recv())
    for block in range(MEMBERS):
        k0[pl.ds(OWN * block, OWN), :] = kr[block, pl.ds(0, OWN), :]
        k1[pl.ds(OWN * block, OWN), :] = kr[block, pl.ds(OWN, OWN), :]
    widen(fr)
    for m in range(OWN):
        spectral = dot(leg[m], mode_in(m))
        spec[m] = spectral
        real, imag = spectral[:, :HALF], spectral[:, HALF:]
        filtered = jnp.concatenate(
            [k0[...] * real - k1[...] * imag, k0[...] * imag + k1[...] * real], axis=1
        ).astype(BF)
        mode_out(m, dot(legt[m], filtered))
    narrow(bs)
    for ch in range(CHUNKS):
        send_site(bs, br, z2s, z2r, ch)

    def grid_stage(pair):
        wave = dot(syt_ref[...], unpack_pair(br, pair))
        slopes = []
        for side in range(2):
            value = wave[:, HALF * side : HALF * (side + 1)]
            sig = jax.nn.sigmoid(value)
            j = 2 * pair + side
            ok[j] = (xk[j].astype(F32) + value * sig).astype(BF)
            slope = gk[j].astype(F32) * (sig * (1.0 + value * (1.0 - sig)))
            slopes.append(slope.astype(BF))
        pack_pair(dot(sy_ref[...], jnp.concatenate(slopes, axis=1)), gs, pair)

    for ch in range(CHUNKS):
        take_grid(g_hbm, gk, cs, cr, ch, grid_in_own, grid_in)
    for ch in range(CHUNKS):
        take_site(bs, br, z2s, z2r, ch)
        pairs_of(ch, grid_stage)
        send_site(gs, gr, z3s, z3r, ch)
        send_grid(ok, out_hbm, os_, or_, ch, grid_out_own, grid_out)

    for ch in range(CHUNKS):
        take_site(gs, gr, z3s, z3r, ch)
    widen(gr)
    t0[...] = jnp.zeros_like(t0)
    t1[...] = jnp.zeros_like(t1)
    weights = jnp.concatenate([wc_ref[...], wc_ref[...]], axis=1)
    for m in range(OWN):
        grad = dot(leg[m], mode_in(m))
        spectral = spec[m]
        real, imag = spectral[:, :HALF], spectral[:, HALF:]
        greal, gimag = grad[:, :HALF], grad[:, HALF:]
        t0[...] += greal * real + gimag * imag
        t1[...] += gimag * real - greal * imag
        coeff = jnp.concatenate(
            [k0[...] * greal + k1[...] * gimag, k0[...] * gimag - k1[...] * greal], axis=1
        ).astype(BF)
        mode_out(m, dot(legt[m], coeff) * weights)
    for block in range(SITES):
        ts[block % 2, block // 2, pl.ds(0, OWN), :] = t0[pl.ds(OWN * block, OWN), :]
        ts[block % 2, block // 2, pl.ds(OWN, OWN), :] = t1[pl.ds(OWN * block, OWN), :]

    def pair_copy():
        return pltpu.make_async_remote_copy(
            src_ref=ts.at[1 - q], dst_ref=tp, send_sem=tps.at[0], recv_sem=tpr.at[0],
            device_id=place(lat, 2 * y + (1 - q)), device_id_type=MESH,
        )

    def terms_copy(i):
        lat_to = lax.rem(lat + i, LATS)
        return pltpu.make_async_remote_copy(
            src_ref=tq.at[lat_to], dst_ref=tr.at[lat],
            send_sem=tcs.at[i], recv_sem=tcr.at[i],
            device_id=place(lat_to, lon), device_id_type=MESH,
        )

    pair_copy().start()
    narrow(hs)
    send_site(hs, hr, z4s, z4r, 0)
    pair_copy().wait_recv()
    tq[...] = ts[q] + tp[...]
    each(1, LATS, lambda i: terms_copy(i).start())
    tr[lat] = tq[lat]
    for ch in range(1, CHUNKS):
        send_site(hs, hr, z4s, z4r, ch)

    def degree_copy():
        return pltpu.make_async_remote_copy(
            src_ref=tb, dst_ref=td.at[member], send_sem=tds.at[0], recv_sem=tdr.at[member],
            device_id={"member": site}, device_id_type=MESH,
        )

    def channel_copy(i):
        lat_to, lon_to = (LATS // 2) * y + lax.div(i, LONS), lax.rem(i, LONS)
        return pltpu.make_async_remote_copy(
            src_ref=fin, dst_ref=te, send_sem=tes.at[i], recv_sem=ter.at[0],
            device_id=place(lat_to, lon_to), device_id_type=MESH,
        )

    def is_self(i):
        return jnp.logical_and(
            (LATS // 2) * y + lax.div(i, LONS) == lat, lax.rem(i, LONS) == lon
        )

    def terms_to_member():
        each(1, LATS, lambda i: terms_copy(i).wait_recv())
        tb[...] = jnp.sum(tr[...], axis=0)

        @pl.when(member != site)
        def _():
            degree_copy().start()

        @pl.when(collects)
        def _():
            td[member] = tb[...]

    def terms_to_owner():
        @pl.when(collects)
        def _():
            def arrive(o):
                @pl.when(o != member)
                def _():
                    pltpu.make_async_remote_copy(
                        src_ref=tb, dst_ref=td.at[o], send_sem=tds.at[0], recv_sem=tdr.at[o],
                        device_id=place(lat, lon), device_id_type=MESH,
                    ).wait_recv()

            each(0, MEMBERS, arrive)
            fin[...] = jnp.sum(td[...], axis=0) * (1.0 / MEMBERS)

            def spread(i):
                @pl.when(jnp.logical_not(is_self(i)))
                def _():
                    channel_copy(i).start()

                @pl.when(is_self(i))
                def _():
                    te[...] = fin[...]

            each(0, SITES, spread)

    def terms_finish():
        @pl.when(jnp.logical_not(collector_is_self))
        def _():
            channel_copy(0).wait_recv()

        for part in range(2):
            fg_ref[part] = lax.dot_general(
                select, te[pl.ds(part * OWN, OWN), :], (((1,), (1,)), ((), ())),
                precision=lax.Precision.HIGHEST, preferred_element_type=F32,
            )

    def last_stage(pair):
        field = dot(ant_ref[...], unpack_pair(hr, pair))
        for side in range(2):
            j = 2 * pair + side
            go[j] = (gk[j].astype(F32) + field[:, HALF * side : HALF * (side + 1)]).astype(BF)

    for ch in range(CHUNKS):
        take_site(hs, hr, z4s, z4r, ch)
        pairs_of(ch, last_stage)
        send_grid(go, gin_hbm, ps, pr, ch, grid_out_own, grid_out)
        if ch == 1:
            terms_to_member()
        if ch == CHUNKS - 1:
            terms_to_owner()
    terms_finish()

    for ch in range(CHUNKS):
        take_grid(ok, out_hbm, os_, or_, ch, grid_out_own, grid_out)
        take_grid(go, gin_hbm, ps, pr, ch, grid_out_own, grid_out)

    for ch in range(CHUNKS):
        each(1, LONS, lambda i: grid_in(x_hbm, xk, xs, xr, ch, i).wait_send())
        each(1, LONS, lambda i: grid_in(g_hbm, gk, cs, cr, ch, i).wait_send())
        each(1, LONS, lambda i: grid_out(ok, out_hbm, os_, or_, ch, i).wait_send())
        each(1, LONS, lambda i: grid_out(go, gin_hbm, ps, pr, ch, i).wait_send())
        each(1, SITES, lambda i: site_copy(fs, fr, z1s, z1r, ch, i).wait_send())
        each(1, SITES, lambda i: site_copy(bs, br, z2s, z2r, ch, i).wait_send())
        each(1, SITES, lambda i: site_copy(gs, gr, z3s, z3r, ch, i).wait_send())
        each(1, SITES, lambda i: site_copy(hs, hr, z4s, z4r, ch, i).wait_send())
    @pl.when(jnp.logical_not(collector_is_self))
    def _():
        owner_copy().wait_send()

    @pl.when(collects)
    def _():
        each(1, MEMBERS, lambda i: member_copy(i).wait_send())

    each(1, SITES, lambda i: degrees_copy(i).wait_send())
    each(1, LATS, lambda i: terms_copy(i).wait_send())
    pair_copy().wait_send()

    @pl.when(member != site)
    def _():
        degree_copy().wait_send()

    @pl.when(collects)
    def _():
        def left(i):
            @pl.when(jnp.logical_not(is_self(i)))
            def _():
                channel_copy(i).wait_send()

        each(0, SITES, left)


def on_device(members_in, cotangent, spectral_filter):
    vmem = pl.BlockSpec(memory_space=pltpu.VMEM)
    anywhere = pl.BlockSpec(memory_space=pl.ANY)
    block = members_in.shape[1:]
    grid_buf = pltpu.VMEM((OWN, NLON, HALF), BF)
    site_buf = pltpu.VMEM((SITES, SROWS, HALF), BF)
    small = pltpu.VMEM((PACK, HALF), F32)
    many = pltpu.VMEM((SITES, PACK, HALF), F32)
    plane = pltpu.VMEM((DEGREES, HALF), F32)
    flat = pltpu.VMEM((SITES * SROWS, HALF), F32)
    table = pltpu.VMEM((OWN, DEGREES, NLAT), BF)
    grid_sem = pltpu.SemaphoreType.DMA((CHUNKS, LONS))
    site_sem = pltpu.SemaphoreType.DMA((CHUNKS, SITES))
    many_sem = pltpu.SemaphoreType.DMA((SITES,))
    one_sem = pltpu.SemaphoreType.DMA((1,))
    scratch = (
        [grid_buf] * 4
        + [site_buf] * 8
        + [flat] * 2
        + [pltpu.VMEM((OWN, DEGREES, 2 * HALF), F32)]
        + [table] * 2
        + [pltpu.VMEM((2, DEGREES * 16, HALF), F32)]
        + [pltpu.VMEM((2, HALF), F32), pltpu.VMEM((SITES, 2, HALF), F32), small, many]
        + [plane] * 4
        + [pltpu.VMEM((2, LATS, PACK, HALF), F32)]
        + [pltpu.VMEM((LATS, PACK, HALF), F32)] * 3
        + [small, many, small, small]
        + [grid_sem] * 8
        + [site_sem] * 8
        + [many_sem] * 6
        + [one_sem, many_sem, many_sem, one_sem, one_sem, one_sem, many_sem, many_sem]
    )
    outputs, grads, filter_grad = pl.pallas_call(
        kernel,
        out_shape=(
            pltpu.VMEM(block, BF),
            pltpu.VMEM(block, BF),
            jax.ShapeDtypeStruct((2, 8, OWN), F32),
        ),
        in_specs=[anywhere, anywhere] + [vmem] * 9,
        out_specs=(vmem, vmem, vmem),
        scratch_shapes=scratch,
        compiler_params=pltpu.CompilerParams(
            collective_id=0, has_side_effects=True, vmem_limit_bytes=56 * 1024 * 1024
        ),
        name="sphere",
    )(
        members_in[0], cotangent[0], jnp.swapaxes(spectral_filter, 1, 2),
        *fourier_constants(), *sphere_constants(),
    )
    return outputs[None], grads[None], jnp.swapaxes(filter_grad, 1, 2)


def solution(mesh):
    placed = (
        P("member", "lat", "lon", None),
        P("member", "lat", "lon", None),
        P(None, "member", ("lat", "lon")),
    )
    return jax.shard_map(
        on_device, mesh=mesh, in_specs=placed, out_specs=placed, check_vma=False
    )
```

```python
import functools
import math

import jax
import jax.numpy as jnp
import ml_dtypes
import numpy as np
from jax import lax
from jax.experimental import pallas as pl
from jax.experimental.pallas import tpu as pltpu
from jax.sharding import PartitionSpec as P

NLAT = 192
NLON = 384
MODES = 192
DEGREES = 192
CHANNELS = 256
MESH = pl.DeviceIdType.MESH
BF = jnp.bfloat16
F32 = jnp.float32

LATS = 8
LONS = 4
MEMBERS = 16
SITES = 16
OWN = 12
PACK = 2 * OWN
HALF = 128
COLS = NLON // LONS
CHUNKS = 6
KMIX = 1
STEP = OWN // CHUNKS
CROWS = STEP * PACK
SROWS = OWN * PACK


def fourier_constants():
    phases = (np.arange(MODES)[:, None] * np.arange(NLON)[None, :] % NLON) * (2.0 * np.pi / NLON)
    cosines, sines = np.cos(phases), np.sin(phases)
    factor = np.where(np.arange(MODES) == 0, 1.0, 2.0)[:, None]
    analysis = np.stack([cosines, -sines]) * (2.0 * np.pi / NLON)
    synthesis = np.stack([factor * cosines, -factor * sines])

    def ordered(table):
        parts = table.astype(np.float32).reshape(2, SITES, OWN, NLON)
        return parts.transpose(1, 0, 2, 3).reshape(2 * MODES, NLON).astype(ml_dtypes.bfloat16)

    analysis, synthesis = ordered(analysis), ordered(synthesis)
    return analysis, np.ascontiguousarray(analysis.T), synthesis, np.ascontiguousarray(synthesis.T)


def sphere_constants():
    theta = (np.arange(NLAT) + 0.5) * (np.pi / NLAT)
    weights = (np.sin(theta) * (np.pi / NLAT)).astype(np.float32)
    by_pair = np.repeat(weights.reshape(NLAT // 2, 2), HALF, axis=1)
    by_row = np.repeat(weights[:, None], HALF, axis=1)
    angles = np.zeros((8, 256), np.float32)
    angles[0, :NLAT] = np.cos(theta)
    angles[1, :NLAT] = np.log(np.sin(theta))
    norms = np.zeros((SITES, 16, HALF), np.float32)
    for order in range(MODES):
        log_norm = 0.5 * math.log((2.0 * order + 1.0) / (4.0 * math.pi)) + 0.5 * (
            math.lgamma(order + 0.5) - math.lgamma(order + 1.0) - 0.5 * math.log(math.pi)
        )
        norms[order // OWN, order % OWN, :] = log_norm
    return by_pair, by_row, angles, norms


def kernel(
    x_hbm, g_hbm, kf_ref, an_ref, ant_ref, sy_ref, syt_ref, wl_ref, wc_ref, ang_ref, nrm_ref,
    out_hbm, gin_hbm, fg_ref,
    xk, gk, ok, go, fs, fr, bs, br, gs, gr, hs, hr, wide, wideb, spec, leg, legt, pf,
    ksend, ka, kb, kr, k0, k1, t0, t1, ts, tp, tq, tr, tb, td, fin, te,
    xs, xr, cs, cr, os_, or_, ps, pr, z1s, z1r, z2s, z2r, z3s, z3r, z4s, z4r,
    kas, kar, kbs, kbr, tcs, tcr, tds, tdr, tes, ter, tps, tpr, kcs, kcr,
):
    member, lat, lon = lax.axis_index("member"), lax.axis_index("lat"), lax.axis_index("lon")
    y, q = lax.div(lon, 2), lax.rem(lon, 2)
    site = 2 * lat + q
    yoff = pl.multiple_of(HALF * y, HALF)

    def each(start, stop, body):
        def step(i, carry):
            body(i)
            return carry

        lax.fori_loop(start, stop, step, 0)

    def place(lat_to, lon_to):
        return {"lat": lat_to, "lon": lon_to}

    def site_peer(i):
        back = SITES - i
        hop, dq = lax.div(back, 2), lax.rem(back, 2)
        odd = lax.rem(hop, 2)
        dz = odd * lax.div(hop + 1, 2) + (1 - odd) * (LATS - lax.div(hop, 2))
        return lax.rem(lat + dz, LATS), lax.rem(q + dq, 2)

    bar = pltpu.get_barrier_semaphore()

    def greet(i):
        to = place(lax.rem(lat + lax.div(i, LONS), LATS), lax.rem(lon + lax.rem(i, LONS), LONS))
        pl.semaphore_signal(bar, inc=1, device_id=to, device_id_type=MESH)

    def greet_member(i):
        to = {"member": lax.rem(member + i, MEMBERS)}
        pl.semaphore_signal(bar, inc=1, device_id=to, device_id_type=MESH)

    each(1, LATS * LONS, greet)
    each(1, MEMBERS, greet_member)
    pl.semaphore_wait(bar, LATS * LONS - 1 + MEMBERS - 1)

    def grid_in(src, dst, ssem, rsem, ch, i):
        lon_to = lax.rem(lon + i, LONS)
        y_to, q_to = lax.div(lon_to, 2), lax.rem(lon_to, 2)
        part = src.at[
            pl.ds(OWN * q_to + STEP * ch, STEP), :, pl.ds(pl.multiple_of(HALF * y_to, HALF), HALF)
        ]
        rows = pl.ds(pl.multiple_of(COLS * lon, COLS), COLS)
        return pltpu.make_async_remote_copy(
            src_ref=part, dst_ref=dst.at[pl.ds(STEP * ch, STEP), rows, :],
            send_sem=ssem.at[ch, i], recv_sem=rsem.at[ch, i],
            device_id=place(lat, lon_to), device_id_type=MESH,
        )

    def grid_in_own(src, dst, sem, ch):
        rows = pl.ds(pl.multiple_of(COLS * lon, COLS), COLS)
        return pltpu.make_async_copy(
            src.at[pl.ds(OWN * q + STEP * ch, STEP), :, pl.ds(yoff, HALF)],
            dst.at[pl.ds(STEP * ch, STEP), rows, :],
            sem.at[ch, 0],
        )

    def grid_out(src, dst, ssem, rsem, ch, i):
        lon_to = lax.rem(lon + i, LONS)
        rows = pl.ds(pl.multiple_of(COLS * lon_to, COLS), COLS)
        return pltpu.make_async_remote_copy(
            src_ref=src.at[pl.ds(STEP * ch, STEP), rows, :],
            dst_ref=dst.at[pl.ds(OWN * q + STEP * ch, STEP), :, pl.ds(yoff, HALF)],
            send_sem=ssem.at[ch, i], recv_sem=rsem.at[ch, i],
            device_id=place(lat, lon_to), device_id_type=MESH,
        )

    def grid_out_own(src, dst, sem, ch):
        rows = pl.ds(pl.multiple_of(COLS * lon, COLS), COLS)
        return pltpu.make_async_copy(
            src.at[pl.ds(STEP * ch, STEP), rows, :],
            dst.at[pl.ds(OWN * q + STEP * ch, STEP), :, pl.ds(yoff, HALF)],
            sem.at[ch, 0],
        )

    def site_copy(src, dst, ssem, rsem, ch, i):
        lat_to, q_to = site_peer(i)
        rows = pl.ds(CROWS * ch, CROWS)
        return pltpu.make_async_remote_copy(
            src_ref=src.at[2 * lat_to + q_to, rows, :], dst_ref=dst.at[site, rows, :],
            send_sem=ssem.at[ch, i], recv_sem=rsem.at[ch, i],
            device_id=place(lat_to, 2 * y + q_to), device_id_type=MESH,
        )

    def site_own(src, dst, sem, ch):
        rows = pl.ds(CROWS * ch, CROWS)
        return pltpu.make_async_copy(src.at[site, rows, :], dst.at[site, rows, :], sem.at[ch, 0])

    def send_grid(src, dst, ssem, rsem, ch, own, remote):
        each(1, LONS, lambda i: remote(src, dst, ssem, rsem, ch, i).start())
        own(src, dst, rsem, ch).start()

    def take_grid(src, dst, ssem, rsem, ch, own, remote):
        each(1, LONS, lambda i: remote(src, dst, ssem, rsem, ch, i).wait_recv())
        own(src, dst, rsem, ch).wait()

    def send_site(src, dst, ssem, rsem, ch):
        each(1, SITES, lambda i: site_copy(src, dst, ssem, rsem, ch, i).start())
        site_own(src, dst, rsem, ch).start()

    def take_site(src, dst, ssem, rsem, ch):
        each(1, SITES, lambda i: site_copy(src, dst, ssem, rsem, ch, i).wait_recv())
        site_own(src, dst, rsem, ch).wait()

    y_own = lax.div(lat, LATS // 2)
    slot = lax.rem(lat, LATS // 2) * LONS + lon
    def exact(a, b, dims):
        return lax.dot_general(
            a, b, (dims, ((), ())), precision=lax.Precision.HIGHEST, preferred_element_type=F32
        )

    def iota(shape, dim):
        return lax.broadcasted_iota(jnp.int32, shape, dim)

    degree_rows = (lax.div(iota((OWN, HALF), 1), 8) == iota((OWN, HALF), 0)).astype(F32)
    channel_rows = lax.rem(iota((8, HALF), 1), 8) == iota((8, HALF), 0)
    for part in range(2):
        spread = exact(kf_ref[part], degree_rows, ((1,), (0,)))
        ksend[pl.ds(part, 1), :] = jnp.sum(
            jnp.where(channel_rows, spread, 0.0), axis=0, keepdims=True
        )
    select = (iota((8, HALF), 1) == 8 * slot + iota((8, HALF), 0)).astype(F32)

    collects = member == site
    collector_is_self = jnp.logical_and(
        lax.div(member, 2) == lat, 2 * y_own + lax.rem(member, 2) == lon
    )

    def owner_copy():
        return pltpu.make_async_remote_copy(
            src_ref=ksend, dst_ref=ka.at[slot], send_sem=kas.at[0], recv_sem=kar.at[slot],
            device_id=place(lax.div(member, 2), 2 * y_own + lax.rem(member, 2)),
            device_id_type=MESH,
        )

    @pl.when(collector_is_self)
    def _():
        ka[slot] = ksend[...]

    @pl.when(jnp.logical_not(collector_is_self))
    def _():
        owner_copy().start()

    for ch in range(2):
        send_grid(x_hbm, xk, xs, xr, ch, grid_in_own, grid_in)

    def owner_wait(o):
        @pl.when(jnp.logical_or(y_own != y, o != slot))
        def _():
            pltpu.make_async_remote_copy(
                src_ref=ksend, dst_ref=ka.at[o], send_sem=kas.at[0], recv_sem=kar.at[o],
                device_id=place(lat, lon), device_id_type=MESH,
            ).wait_recv()

    def member_copy(i):
        return pltpu.make_async_remote_copy(
            src_ref=kb, dst_ref=kr.at[member], send_sem=kbs.at[i], recv_sem=kbr.at[0],
            device_id={"member": lax.rem(member + i, MEMBERS)}, device_id_type=MESH,
        )

    def degrees_copy(i):
        lat_to, q_to = site_peer(i)
        return pltpu.make_async_remote_copy(
            src_ref=kr.at[site], dst_ref=kr.at[site], send_sem=kcs.at[i], recv_sem=kcr.at[i],
            device_id=place(lat_to, 2 * y + q_to), device_id_type=MESH,
        )

    @pl.when(collects)
    def _():
        each(0, SITES, owner_wait)
        owner_rows = (lax.div(iota((HALF, SITES), 0), 8) == iota((HALF, SITES), 1)).astype(F32)
        own_lanes = lax.rem(iota((HALF, HALF), 1), 8) == lax.rem(iota((HALF, HALF), 0), 8)
        for part in range(2):
            rows = jnp.concatenate([ka[o, pl.ds(part, 1), :] for o in range(SITES)], axis=0)
            spread = jnp.where(own_lanes, exact(owner_rows, rows, ((1,), (0,))), 0.0)
            kb[pl.ds(part * OWN, OWN), :] = exact(degree_rows, spread, ((1,), (1,)))
        each(1, MEMBERS, lambda i: member_copy(i).start())
        kr[member] = kb[...]

    def degrees_to_sites():
        @pl.when(jnp.logical_not(collects))
        def _():
            member_copy(1).wait_recv()

        each(1, SITES, lambda i: degrees_copy(i).start())

    for ch in range(2, CHUNKS):
        send_grid(x_hbm, xk, xs, xr, ch, grid_in_own, grid_in)

    orders = (OWN * site + lax.broadcasted_iota(jnp.int32, (16, HALF), 0)).astype(F32)
    squares = orders * orders
    cosine = [ang_ref[pl.ds(0, 1), pl.ds(HALF * h, HALF)] for h in range(2)]
    logsin = [ang_ref[pl.ds(1, 1), pl.ds(HALF * h, HALF)] for h in range(2)]
    diagonal = [jnp.exp(nrm_ref[site] + orders * logsin[h]) for h in range(2)]

    def degree_step(l, carry):
        degree = jnp.full((16, HALF), l, jnp.int32).astype(F32)
        before = degree - 1.0
        upward = jnp.sqrt(
            jnp.maximum(4.0 * degree * degree - 1.0, 1.0)
            / jnp.maximum(degree * degree - squares, 1.0)
        )
        damping = jnp.sqrt(
            jnp.maximum(before * before - squares, 0.0)
            / jnp.maximum(4.0 * before * before - 1.0, 1.0)
        )
        state = []
        for h in range(2):
            earlier, latest = carry[2 * h], carry[2 * h + 1]
            recurred = upward * (cosine[h] * latest - damping * earlier)
            updated = jnp.where(
                degree == orders, diagonal[h], jnp.where(degree > orders, recurred, 0.0)
            )
            pf[h, pl.ds(pl.multiple_of(16 * l, 16), 16), :] = updated
            state += [latest, updated]
        return tuple(state)

    start = tuple(diagonal[h] * 0.0 for h in (0, 0, 1, 1))
    lax.fori_loop(0, DEGREES, degree_step, start, unroll=4)
    for m in range(OWN):
        table = jnp.concatenate(
            [pf[h, pl.ds(m, DEGREES, stride=16), :] for h in range(2)], axis=1
        )
        leg[m] = table[:, :NLAT].astype(BF)
        legt[m] = jnp.transpose(table)[:NLAT].astype(BF)

    def pack_pair(values, ref, pair):
        rows = pl.ds(pl.multiple_of(2 * PACK * pair, 2 * PACK), 2 * PACK)
        for d in range(SITES):
            block = values[PACK * d : PACK * (d + 1)]
            ref[d, rows, :] = jnp.concatenate([block[:, :HALF], block[:, HALF:]], axis=0).astype(BF)

    def unpack_pair(ref, pair):
        rows = pl.ds(pl.multiple_of(2 * PACK * pair, 2 * PACK), 2 * PACK)
        blocks = [ref[d, rows, :].astype(F32) for d in range(SITES)]
        first = jnp.concatenate([block[:PACK] for block in blocks], axis=0).astype(BF)
        second = jnp.concatenate([block[PACK:] for block in blocks], axis=0).astype(BF)
        return jnp.concatenate([first, second], axis=1)

    def dot(a, b):
        return jnp.dot(a, b, preferred_element_type=F32)

    def pairs_of(ch, body):
        each(ch * (STEP // 2), (ch + 1) * (STEP // 2), body)

    def analyse(pair):
        field = jnp.concatenate([xk[2 * pair], xk[2 * pair + 1]], axis=1)
        weight = wl_ref[pl.ds((OWN // 2) * site + pair, 1), :]
        pack_pair(dot(an_ref[...], field) * weight, fs, pair)

    for ch in range(CHUNKS):
        take_grid(x_hbm, xk, xs, xr, ch, grid_in_own, grid_in)
        pairs_of(ch, analyse)
        send_site(fs, fr, z1s, z1r, ch)
        if ch == KMIX:
            degrees_to_sites()
    for ch in range(CHUNKS):
        send_grid(g_hbm, gk, cs, cr, ch, grid_in_own, grid_in)

    def widen(ref):
        for d in range(SITES):
            wide[pl.ds(SROWS * d, SROWS), :] = ref[d].astype(F32)

    def narrow(ref):
        for d in range(SITES):
            ref[d] = wideb[pl.ds(SROWS * d, SROWS), :].astype(BF)

    def mode_in(m):
        return jnp.concatenate(
            [wide[pl.ds(part * OWN + m, NLAT, stride=PACK), :] for part in range(2)], axis=1
        ).astype(BF)

    def mode_out(m, values):
        for part in range(2):
            wideb[pl.ds(part * OWN + m, NLAT, stride=PACK), :] = values[
                :, HALF * part : HALF * (part + 1)
            ]

    for ch in range(CHUNKS):
        take_site(fs, fr, z1s, z1r, ch)
    each(1, SITES, lambda i: degrees_copy(i).wait_recv())
    for block in range(MEMBERS):
        k0[pl.ds(OWN * block, OWN), :] = kr[block, pl.ds(0, OWN), :]
        k1[pl.ds(OWN * block, OWN), :] = kr[block, pl.ds(OWN, OWN), :]
    widen(fr)
    for m in range(OWN):
        spectral = dot(leg[m], mode_in(m))
        spec[m] = spectral
        real, imag = spectral[:, :HALF], spectral[:, HALF:]
        filtered = jnp.concatenate(
            [k0[...] * real - k1[...] * imag, k0[...] * imag + k1[...] * real], axis=1
        ).astype(BF)
        mode_out(m, dot(legt[m], filtered))
    narrow(bs)
    for ch in range(CHUNKS):
        send_site(bs, br, z2s, z2r, ch)

    def grid_stage(pair):
        wave = dot(syt_ref[...], unpack_pair(br, pair))
        slopes = []
        for side in range(2):
            value = wave[:, HALF * side : HALF * (side + 1)]
            sig = jax.nn.sigmoid(value)
            j = 2 * pair + side
            ok[j] = (xk[j].astype(F32) + value * sig).astype(BF)
            slope = gk[j].astype(F32) * (sig * (1.0 + value * (1.0 - sig)))
            slopes.append(slope.astype(BF))
        pack_pair(dot(sy_ref[...], jnp.concatenate(slopes, axis=1)), gs, pair)

    for ch in range(CHUNKS):
        take_grid(g_hbm, gk, cs, cr, ch, grid_in_own, grid_in)
    for ch in range(CHUNKS):
        take_site(bs, br, z2s, z2r, ch)
        pairs_of(ch, grid_stage)
        send_site(gs, gr, z3s, z3r, ch)
        send_grid(ok, out_hbm, os_, or_, ch, grid_out_own, grid_out)

    for ch in range(CHUNKS):
        take_site(gs, gr, z3s, z3r, ch)
    widen(gr)
    t0[...] = jnp.zeros_like(t0)
    t1[...] = jnp.zeros_like(t1)
    weights = jnp.concatenate([wc_ref[...], wc_ref[...]], axis=1)
    for m in range(OWN):
        grad = dot(leg[m], mode_in(m))
        spectral = spec[m]
        real, imag = spectral[:, :HALF], spectral[:, HALF:]
        greal, gimag = grad[:, :HALF], grad[:, HALF:]
        t0[...] += greal * real + gimag * imag
        t1[...] += gimag * real - greal * imag
        coeff = jnp.concatenate(
            [k0[...] * greal + k1[...] * gimag, k0[...] * gimag - k1[...] * greal], axis=1
        ).astype(BF)
        mode_out(m, dot(legt[m], coeff) * weights)
    for block in range(SITES):
        ts[block % 2, block // 2, pl.ds(0, OWN), :] = t0[pl.ds(OWN * block, OWN), :]
        ts[block % 2, block // 2, pl.ds(OWN, OWN), :] = t1[pl.ds(OWN * block, OWN), :]

    def pair_copy():
        return pltpu.make_async_remote_copy(
            src_ref=ts.at[1 - q], dst_ref=tp, send_sem=tps.at[0], recv_sem=tpr.at[0],
            device_id=place(lat, 2 * y + (1 - q)), device_id_type=MESH,
        )

    def terms_copy(i):
        lat_to = lax.rem(lat + i, LATS)
        return pltpu.make_async_remote_copy(
            src_ref=tq.at[lat_to], dst_ref=tr.at[lat],
            send_sem=tcs.at[i], recv_sem=tcr.at[i],
            device_id=place(lat_to, lon), device_id_type=MESH,
        )

    pair_copy().start()
    narrow(hs)
    send_site(hs, hr, z4s, z4r, 0)
    pair_copy().wait_recv()
    tq[...] = ts[q] + tp[...]
    each(1, LATS, lambda i: terms_copy(i).start())
    tr[lat] = tq[lat]
    for ch in range(1, CHUNKS):
        send_site(hs, hr, z4s, z4r, ch)

    def degree_copy():
        return pltpu.make_async_remote_copy(
            src_ref=tb, dst_ref=td.at[member], send_sem=tds.at[0], recv_sem=tdr.at[member],
            device_id={"member": site}, device_id_type=MESH,
        )

    def channel_copy(i):
        lat_to, lon_to = (LATS // 2) * y + lax.div(i, LONS), lax.rem(i, LONS)
        return pltpu.make_async_remote_copy(
            src_ref=fin, dst_ref=te, send_sem=tes.at[i], recv_sem=ter.at[0],
            device_id=place(lat_to, lon_to), device_id_type=MESH,
        )

    def is_self(i):
        return jnp.logical_and(
            (LATS // 2) * y + lax.div(i, LONS) == lat, lax.rem(i, LONS) == lon
        )

    def terms_to_member():
        each(1, LATS, lambda i: terms_copy(i).wait_recv())
        tb[...] = jnp.sum(tr[...], axis=0)

        @pl.when(member != site)
        def _():
            degree_copy().start()

        @pl.when(collects)
        def _():
            td[member] = tb[...]

    def terms_to_owner():
        @pl.when(collects)
        def _():
            def arrive(o):
                @pl.when(o != member)
                def _():
                    pltpu.make_async_remote_copy(
                        src_ref=tb, dst_ref=td.at[o], send_sem=tds.at[0], recv_sem=tdr.at[o],
                        device_id=place(lat, lon), device_id_type=MESH,
                    ).wait_recv()

            each(0, MEMBERS, arrive)
            fin[...] = jnp.sum(td[...], axis=0) * (1.0 / MEMBERS)

            def spread(i):
                @pl.when(jnp.logical_not(is_self(i)))
                def _():
                    channel_copy(i).start()

                @pl.when(is_self(i))
                def _():
                    te[...] = fin[...]

            each(0, SITES, spread)

    def terms_finish():
        @pl.when(jnp.logical_not(collector_is_self))
        def _():
            channel_copy(0).wait_recv()

        for part in range(2):
            fg_ref[part] = lax.dot_general(
                select, te[pl.ds(part * OWN, OWN), :], (((1,), (1,)), ((), ())),
                precision=lax.Precision.HIGHEST, preferred_element_type=F32,
            )

    def last_stage(pair):
        field = dot(ant_ref[...], unpack_pair(hr, pair))
        for side in range(2):
            j = 2 * pair + side
            go[j] = (gk[j].astype(F32) + field[:, HALF * side : HALF * (side + 1)]).astype(BF)

    for ch in range(CHUNKS):
        take_site(hs, hr, z4s, z4r, ch)
        pairs_of(ch, last_stage)
        send_grid(go, gin_hbm, ps, pr, ch, grid_out_own, grid_out)
        if ch == 1:
            terms_to_member()
        if ch == CHUNKS - 1:
            terms_to_owner()
    terms_finish()

    for ch in range(CHUNKS):
        take_grid(ok, out_hbm, os_, or_, ch, grid_out_own, grid_out)
        take_grid(go, gin_hbm, ps, pr, ch, grid_out_own, grid_out)

    for ch in range(CHUNKS):
        each(1, LONS, lambda i: grid_in(x_hbm, xk, xs, xr, ch, i).wait_send())
        each(1, LONS, lambda i: grid_in(g_hbm, gk, cs, cr, ch, i).wait_send())
        each(1, LONS, lambda i: grid_out(ok, out_hbm, os_, or_, ch, i).wait_send())
        each(1, LONS, lambda i: grid_out(go, gin_hbm, ps, pr, ch, i).wait_send())
        each(1, SITES, lambda i: site_copy(fs, fr, z1s, z1r, ch, i).wait_send())
        each(1, SITES, lambda i: site_copy(bs, br, z2s, z2r, ch, i).wait_send())
        each(1, SITES, lambda i: site_copy(gs, gr, z3s, z3r, ch, i).wait_send())
        each(1, SITES, lambda i: site_copy(hs, hr, z4s, z4r, ch, i).wait_send())
    @pl.when(jnp.logical_not(collector_is_self))
    def _():
        owner_copy().wait_send()

    @pl.when(collects)
    def _():
        each(1, MEMBERS, lambda i: member_copy(i).wait_send())

    each(1, SITES, lambda i: degrees_copy(i).wait_send())
    each(1, LATS, lambda i: terms_copy(i).wait_send())
    pair_copy().wait_send()

    @pl.when(member != site)
    def _():
        degree_copy().wait_send()

    @pl.when(collects)
    def _():
        def left(i):
            @pl.when(jnp.logical_not(is_self(i)))
            def _():
                channel_copy(i).wait_send()

        each(0, SITES, left)


def on_device(members_in, cotangent, spectral_filter):
    vmem = pl.BlockSpec(memory_space=pltpu.VMEM)
    anywhere = pl.BlockSpec(memory_space=pl.ANY)
    block = members_in.shape[1:]
    grid_buf = pltpu.VMEM((OWN, NLON, HALF), BF)
    site_buf = pltpu.VMEM((SITES, SROWS, HALF), BF)
    small = pltpu.VMEM((PACK, HALF), F32)
    many = pltpu.VMEM((SITES, PACK, HALF), F32)
    plane = pltpu.VMEM((DEGREES, HALF), F32)
    flat = pltpu.VMEM((SITES * SROWS, HALF), F32)
    table = pltpu.VMEM((OWN, DEGREES, NLAT), BF)
    grid_sem = pltpu.SemaphoreType.DMA((CHUNKS, LONS))
    site_sem = pltpu.SemaphoreType.DMA((CHUNKS, SITES))
    many_sem = pltpu.SemaphoreType.DMA((SITES,))
    one_sem = pltpu.SemaphoreType.DMA((1,))
    scratch = (
        [grid_buf] * 4
        + [site_buf] * 8
        + [flat] * 2
        + [pltpu.VMEM((OWN, DEGREES, 2 * HALF), F32)]
        + [table] * 2
        + [pltpu.VMEM((2, DEGREES * 16, HALF), F32)]
        + [pltpu.VMEM((2, HALF), F32), pltpu.VMEM((SITES, 2, HALF), F32), small, many]
        + [plane] * 4
        + [pltpu.VMEM((2, LATS, PACK, HALF), F32)]
        + [pltpu.VMEM((LATS, PACK, HALF), F32)] * 3
        + [small, many, small, small]
        + [grid_sem] * 8
        + [site_sem] * 8
        + [many_sem] * 6
        + [one_sem, many_sem, many_sem, one_sem, one_sem, one_sem, many_sem, many_sem]
    )
    outputs, grads, filter_grad = pl.pallas_call(
        kernel,
        out_shape=(
            pltpu.VMEM(block, BF),
            pltpu.VMEM(block, BF),
            jax.ShapeDtypeStruct((2, 8, OWN), F32),
        ),
        in_specs=[anywhere, anywhere] + [vmem] * 9,
        out_specs=(vmem, vmem, vmem),
        scratch_shapes=scratch,
        compiler_params=pltpu.CompilerParams(
            collective_id=0, has_side_effects=True, vmem_limit_bytes=56 * 1024 * 1024
        ),
        name="sphere",
    )(
        members_in[0], cotangent[0], jnp.swapaxes(spectral_filter, 1, 2),
        *fourier_constants(), *sphere_constants(),
    )
    return outputs[None], grads[None], jnp.swapaxes(filter_grad, 1, 2)


def solution(mesh):
    placed = (
        P("member", "lat", "lon", None),
        P("member", "lat", "lon", None),
        P(None, "member", ("lat", "lon")),
    )
    return jax.shard_map(
        on_device, mesh=mesh, in_specs=placed, out_specs=placed, check_vma=False
    )
```
